32 devices in a mesh: rep: 8 (over z, y), feat: 4 (over x, core).
Axes of the slice: x: 2, y: 2, z: 4, core: 2. Of those that a mesh axis runs over, the one named last changes fastest.
Arguments:
- activations: bfloat16 [8192, 8192], P('rep', 'feat'), may hold values from -6 to 6
- out_grad: bfloat16 [8192, 512], P(('rep', 'feat')), may hold values from -6 to 6
- weight: float32 [8192, 512], P('feat'), may hold values from -0.25 to 0.25
- momentum: float32 [8, 8192, 512], P('rep', 'feat'), may hold values from -4 to 4
- select: int32 [8, 32], replicated, may hold values from 0 to 4095, as said below
Outputs:
- input_grad: float32 [8192, 8192], P('rep', 'feat')
- residual: float32 [8, 8192, 512], P('rep', 'feat')
- new_weight: float32 [8192, 512], P('feat')
The draws below stay inside these ranges and needn't reach their ends.
Inputs may be any that keep to these rules, and one draw needn't show every extreme that they name: `select`: each replica's row holds 32 distinct frequency rows.
All inputs are finite; a program needn't handle non-finite values.
Results may differ from the reference program's by a relative error of at most 0.0003.
Values may be sent and summed in bfloat16 or wider, within the bound.
No kernel may reach another device: no remote copies, remote signals or barrier semaphores. Data moves between devices by JAX's collectives and lax.ppermute only.
A program may use at most 128 MiB of HBM per device.

```python
import jax
import jax.numpy as jnp
from jax import lax

D = 8192
KV = 512
CH = 64
K = 32
TOK = 1024
REPS = 8
TOKENS = 8192


def draw_select(key, part):

    def one_row(replica):
        order = jax.random.permutation(jax.random.fold_in(key, replica + 17), CH * CH)
        return order[:K]
    return jax.vmap(one_row)(jnp.arange(REPS)).astype(jnp.int32)


def steps_of(key, extent, split, smallest, high):
    factor_of = 1.0
    for position, blocks in split:
        heights = jax.random.uniform(jax.random.fold_in(jax.random.fold_in(key, 6), position), (blocks,), jnp.float32, smallest / len(split), high / len(split))
        factor_of = factor_of * jnp.repeat(jnp.exp(heights), extent[position] // blocks).reshape((-1,) + (1,) * (len(extent) - 1 - position))
    return factor_of


def gaussian(stream_key, dims, width, reach, pieces=(), held_as=jnp.bfloat16):
    entries = jax.random.normal(stream_key, dims, jnp.float32) * width
    if len(pieces) > 0:
        entries = steps_of(stream_key, dims, pieces, -0.22, 0.18) * entries
    return jnp.clip(entries, min=-reach, max=reach).astype(held_as)


def setup_inputs(seed: int = 0) -> dict:
    key_of = jax.random.split(jax.random.key(seed), 6)
    return {
        "activations": gaussian(key_of[0], (TOKENS, D), 1.0, 6.0, ((0, 8), (1, 4))),
        "out_grad": gaussian(key_of[1], (TOKENS, KV), 1.0, 6.0, ((0, 32),)),
        "weight": gaussian(key_of[2], (D, KV), KV ** -0.5, 0.25, ((0, 4),), jnp.float32),
        "momentum": gaussian(key_of[3], (REPS, D, KV), 0.5, 4.0, ((0, 8), (1, 4)), jnp.float32),
        "select": draw_select(jax.random.fold_in(key_of[5], 71), 0),
    }


momentum_decay = 0.9
step_rate = 0.5

def dct_table():
    index = jnp.arange(CH).astype(jnp.float32)
    table = jnp.cos(jnp.pi * (2.0 * index[None, :] + 1.0) * index[:, None] / (2.0 * CH)) * jnp.sqrt(2.0 / CH)
    first = jnp.where(jnp.arange(CH) == 0, jnp.sqrt(0.5), 1.0).astype(jnp.float32)
    return table * first[:, None]

def forward(field, table):
    blocks = field.reshape(field.shape[0] // CH, CH, field.shape[1] // CH, CH)
    inner = jnp.einsum('iajb,vb->iajv', blocks, table, precision=lax.Precision.HIGHEST)
    coef = jnp.einsum('ua,iajv->uvij', table, inner, precision=lax.Precision.HIGHEST)
    return coef.reshape(CH * CH, -1)

def inverse(coef, nrows, ncols, table):
    blocks = coef.reshape(CH, CH, nrows // CH, ncols // CH)
    inner = jnp.einsum('uvij,vb->uijb', blocks, table, precision=lax.Precision.HIGHEST)
    field = jnp.einsum('ua,uijb->iajb', table, inner, precision=lax.Precision.HIGHEST)
    return field.reshape(nrows, ncols)

def reference(activations, out_grad, weight, momentum, select):
    table = dct_table()

    def one_replica(total, replica):
        x_rows = lax.dynamic_slice_in_dim(activations, replica * TOK, TOK, 0)
        g_rows = lax.dynamic_slice_in_dim(out_grad, replica * TOK, TOK, 0)
        in_grad = jnp.dot(g_rows.astype(jnp.float32), weight.T, precision=lax.Precision.HIGHEST)
        grad = jnp.dot(x_rows.T, g_rows, preferred_element_type=jnp.float32) / TOK
        moment = momentum_decay * momentum[replica] + grad
        coef = forward(moment, table)
        rows = select[replica]
        kept = jnp.zeros_like(coef).at[rows].set(coef[rows])
        back = inverse(kept, D, KV, table)
        return (total + back, (in_grad, moment - back))
    total, (grads, residual) = lax.scan(one_replica, jnp.zeros((D, KV), jnp.float32), jnp.arange(REPS).astype(jnp.int32))
    new_weight = weight - step_rate * total
    return (grads.reshape(REPS * TOK, D), residual, new_weight)
```

```python
import functools
import math

import jax
import jax.numpy as jnp
import numpy as np
from jax import lax
from jax.experimental import pallas as pl
from jax.experimental.pallas import tpu as pltpu
from jax.sharding import PartitionSpec as P

CH = 64
BF = jnp.bfloat16
F32 = jnp.float32

momentum_decay = 0.9
step_rate = 0.5


def dct_thirds():
    index = np.arange(CH, dtype=np.float64)
    table = np.cos(np.pi * (2.0 * index[None, :] + 1.0) * index[:, None] / (2.0 * CH))
    table = table * np.sqrt(2.0 / CH)
    table[0] *= np.sqrt(0.5)
    terms = []
    rest = table.astype(np.float32)
    for _ in range(3):
        term = rest.astype(BF)
        terms.append(term)
        rest = rest - term.astype(np.float32)
    return np.concatenate(terms, axis=0)


def split2(value):
    high = value.astype(BF)
    return high, (value - high.astype(F32)).astype(BF)


def dot(a, b, contract=((1,), (0,))):
    return lax.dot_general(a, b, (contract, ((), ())), preferred_element_type=F32)


def one_hots(row):
    n = row.shape[1]
    freq = lax.broadcasted_iota(jnp.int32, (3 * CH, n), 0) & (CH - 1)
    u = (freq == (row >> int(math.log2(CH)))).astype(F32).astype(BF)
    v = (freq == (row & (CH - 1))).astype(F32).astype(BF)
    return u, v


def table_kernel(order_ref, sel_ref, thirds_ref, high_ref, low_ref, u_ref, v_ref):
    chunk = pl.program_id(0)
    reps, kept = sel_ref.shape
    lanes = high_ref.shape[1]

    @pl.when(chunk == 0)
    def _():
        for p in range(reps):
            u, v = one_hots(sel_ref[pl.ds(order_ref[p], 1), :])
            rows = pl.ds(p * kept, kept)
            uu = dot(u, thirds_ref[...], ((0,), (0,)))
            vv = dot(v, thirds_ref[...], ((0,), (0,)))
            u_high, rest = split2(uu)
            u_mid, _ = split2(rest.astype(F32))
            u_low = (uu - u_high.astype(F32) - u_mid.astype(F32)).astype(BF)
            u_ref[rows, :] = jnp.concatenate([u_high, u_mid, u_low], axis=1)
            v_ref[rows, :] = jnp.concatenate([vv, vv], axis=1)

    row = lax.broadcasted_iota(jnp.int32, (3 * CH, lanes), 0) & (CH - 1)
    col = lax.broadcasted_iota(jnp.int32, (3 * CH, lanes), 1) // CH + chunk * (lanes // CH)
    spread = (row == col).astype(F32).astype(BF)
    wide = dot(u_ref[...], spread) * jnp.concatenate([v_ref[...]] * (lanes // (2 * CH)), axis=1)
    high_ref[...], low_ref[...] = split2(wide)


def make_tables(order, select, thirds, chunk):
    total = select.shape[0] * select.shape[1]
    wide = CH * CH
    lanes = chunk * CH
    return pl.pallas_call(
        table_kernel,
        out_shape=[jax.ShapeDtypeStruct((total, wide), BF)] * 2,
        grid_spec=pltpu.PrefetchScalarGridSpec(
            num_scalar_prefetch=1,
            grid=(wide // lanes,),
            in_specs=[
                pl.BlockSpec(select.shape, lambda c, o: (0, 0)),
                pl.BlockSpec(thirds.shape, lambda c, o: (0, 0)),
            ],
            out_specs=[pl.BlockSpec((total, lanes), lambda c, o: (0, c))] * 2,
            scratch_shapes=[pltpu.VMEM((total, 3 * CH), BF), pltpu.VMEM((total, 2 * CH), F32)],
        ),
        cost_estimate=pl.CostEstimate(
            flops=2 * total * wide * 3 * CH, bytes_accessed=4 * total * wide, transcendentals=0
        ),
        name="tables",
    )(order, select, thirds)


def grad_kernel(
    tokens, where_ref, *refs
):
    pieces = (len(refs) - 10) // 2
    xs, gs = refs[:pieces], refs[pieces : 2 * pieces]
    mom_ref, sel_ref, thirds_ref, res_ref, coef_ref = refs[2 * pieces : 2 * pieces + 5]
    fwd_ref, inv_ref, v_ref, pick_ref, ones_ref = refs[2 * pieces + 5 :]
    step = pl.program_id(0)
    rows, cols = mom_ref.shape[1:]
    group = rows // CH
    kept = sel_ref.shape[1]
    slots = coef_ref.shape[1]
    high = slots // (cols // CH)

    @pl.when(step == 0)
    def _():
        u, v = one_hots(sel_ref[pl.ds(where_ref[0], 1), :])
        uu = dot(u, thirds_ref[...], ((0,), (0,)))
        vv = dot(v, thirds_ref[...], ((0,), (0,)))
        tall = jnp.concatenate([jnp.concatenate([uu] * group, axis=1)] * group, axis=0)
        r = lax.broadcasted_iota(jnp.int32, tall.shape, 0) // kept
        c = lax.broadcasted_iota(jnp.int32, tall.shape, 1) // CH
        tall = jnp.where(r == c, tall, 0.0)
        fwd_high, fwd_low = split2(tall)
        fwd_ref[...] = jnp.concatenate([fwd_high, fwd_low], axis=0)
        inv_high, inv_low = split2(tall.T)
        inv_ref[...] = jnp.concatenate([inv_high, inv_low], axis=0)
        v_ref[...] = jnp.concatenate(
            [jnp.concatenate([vv] * (cols // CH), axis=1)] * group, axis=0
        )
        r = lax.broadcasted_iota(jnp.int32, pick_ref.shape, 0) // CH
        c = lax.broadcasted_iota(jnp.int32, pick_ref.shape, 1) // high
        pick_ref[...] = (r == c).astype(F32).astype(BF)
        r = lax.broadcasted_iota(jnp.int32, ones_ref.shape, 0) // CH
        c = lax.broadcasted_iota(jnp.int32, ones_ref.shape, 1) // CH
        ones_ref[...] = (r == c).astype(F32).astype(BF)
        coef_ref[...] = jnp.zeros_like(coef_ref)

    grad = dot(xs[0][...], gs[0][...], ((0,), (0,)))
    for x, g in zip(xs[1:], gs[1:]):
        grad += dot(x[...], g[...], ((0,), (0,)))
    moment = momentum_decay * mom_ref[0] + grad / tokens
    m_high, m_low = split2(moment)
    half = group * kept
    both = dot(fwd_ref[...], m_high)
    inner = both[:half] + both[half:] + dot(fwd_ref[:half], m_low)
    prod_high, prod_low = split2(inner * v_ref[...])
    packed = dot(prod_high, pick_ref[...]) + dot(prod_low, pick_ref[...])
    lane = lax.broadcasted_iota(jnp.int32, (kept, slots), 1) % high
    own = jnp.zeros((kept, slots), F32)
    for i in range(group):
        own += jnp.where(lane == step * group + i, packed[i * kept : (i + 1) * kept], 0.0)
    coef_ref[...] += own
    width = ones_ref.shape[0]
    wide = []
    for c in range(cols // width):
        part = slice(c * width, (c + 1) * width)
        wide.append(dot(prod_high[:, part], ones_ref[...]) + dot(prod_low[:, part], ones_ref[...]))
    e_high, e_low = split2(jnp.concatenate(wide, axis=1) * v_ref[...])
    back = dot(inv_ref[:rows], e_high) + dot(inv_ref[rows:], e_high) + dot(inv_ref[:rows], e_low)
    res_ref[0] = moment - back


def make_grad(where, activations, pieces, momentum, select, thirds, rows):
    tokens, feats = activations.shape
    cols = momentum.shape[2]
    kept = select.shape[1]
    slots = (feats // CH) * (cols // CH)
    count = len(pieces)
    each = tokens // count
    group = rows // CH
    width = math.gcd(256, cols)

    def x_spec(s):
        return pl.BlockSpec((each, rows), lambda b, w: (w[1 + s], b))

    return pl.pallas_call(
        functools.partial(grad_kernel, tokens),
        out_shape=[
            jax.ShapeDtypeStruct(momentum.shape, F32),
            jax.ShapeDtypeStruct((kept, slots), F32),
        ],
        grid_spec=pltpu.PrefetchScalarGridSpec(
            num_scalar_prefetch=1,
            grid=(feats // rows,),
            in_specs=[x_spec(s) for s in range(count)]
            + [pl.BlockSpec((each, cols), lambda b, w: (0, 0))] * count
            + [
                pl.BlockSpec((1, rows, cols), lambda b, w: (0, b, 0)),
                pl.BlockSpec(select.shape, lambda b, w: (0, 0)),
                pl.BlockSpec(thirds.shape, lambda b, w: (0, 0)),
            ],
            out_specs=[
                pl.BlockSpec((1, rows, cols), lambda b, w: (0, b, 0)),
                pl.BlockSpec((kept, slots), lambda b, w: (0, 0)),
            ],
            scratch_shapes=[
                pltpu.VMEM((2 * group * kept, rows), BF),
                pltpu.VMEM((2 * rows, group * kept), BF),
                pltpu.VMEM((group * kept, cols), F32),
                pltpu.VMEM((cols, slots), BF),
                pltpu.VMEM((width, width), BF),
            ],
        ),
        cost_estimate=pl.CostEstimate(
            flops=2 * tokens * feats * cols * 2,
            bytes_accessed=2 * tokens * feats + 8 * feats * cols,
            transcendentals=0,
        ),
        name="grad",
    )(where, *([activations] * count), *pieces, momentum, select, thirds)


def in_grad_kernel(pieces, where_ref, *refs):
    gs = refs[:pieces]
    w_ref = refs[pieces]
    out_ref = refs[-1]
    w_high, w_low = split2(w_ref[...])
    each = gs[0].shape[0]
    for s in range(pieces):
        at = pl.multiple_of(where_ref[1 + s] * each, each)
        g = gs[s][...]
        out_ref[pl.ds(at, each), :] = dot(g, w_high, ((1,), (1,))) + dot(g, w_low, ((1,), (1,)))


def make_in_grad(where, pieces, weight, before, rows):
    feats, cols = weight.shape
    count = len(pieces)
    each = pieces[0].shape[0]
    shape, prior = before
    in_specs = [pl.BlockSpec((each, cols), lambda b, w: (0, 0))] * count
    in_specs.append(pl.BlockSpec((rows, cols), lambda b, w: (b, 0)))
    args = [where, *pieces, weight]
    aliases = {}
    if prior is not None:
        in_specs.append(pl.BlockSpec(memory_space=pl.ANY))
        args.append(prior)
        aliases = {len(args) - 1: 0}
    return pl.pallas_call(
        functools.partial(in_grad_kernel, count),
        out_shape=jax.ShapeDtypeStruct(shape, F32),
        grid_spec=pltpu.PrefetchScalarGridSpec(
            num_scalar_prefetch=1,
            grid=(feats // rows,),
            in_specs=in_specs,
            out_specs=pl.BlockSpec((count * each, rows), lambda b, w: (w[0], b)),
        ),
        input_output_aliases=aliases,
        cost_estimate=pl.CostEstimate(
            flops=2 * count * each * feats * cols * 2,
            bytes_accessed=4 * count * each * feats + 4 * feats * cols,
            transcendentals=0,
        ),
        name="in_grad",
    )(*args)


def total_kernel(coef_ref, high_ref, low_ref, w_ref, out_ref, t_high, t_low, sum_ref):
    high, each, cols = w_ref.shape

    @pl.when(pl.program_id(0) == 0)
    def _():
        t_high[...], t_low[...] = split2(coef_ref[...].T)

    total = (
        dot(t_high[...], high_ref[...])
        + dot(t_low[...], high_ref[...])
        + dot(t_high[...], low_ref[...])
    )
    left = lax.broadcasted_iota(jnp.int32, (high, 2 * CH), 1) < CH
    for p in range(each // 2):
        lanes = slice(p * 2 * CH, (p + 1) * 2 * CH)
        for q in range(cols // (2 * CH)):
            even = total[(2 * q) * high : (2 * q + 1) * high, lanes]
            odd = total[(2 * q + 1) * high : (2 * q + 2) * high, lanes]
            first = jnp.where(left, even, pltpu.roll(odd, CH, 1))
            second = jnp.where(left, pltpu.roll(even, CH, 1), odd)
            sum_ref[q, pl.ds(2 * p, high, stride=each), :] = first
            sum_ref[q, pl.ds(2 * p + 1, high, stride=each), :] = second
    for q in range(cols // (2 * CH)):
        at = slice(q * 2 * CH, (q + 1) * 2 * CH)
        out_ref[:, :, at] = w_ref[:, :, at] - step_rate * sum_ref[q].reshape(high, each, 2 * CH)


def make_total(coefs, w_high, w_low, weight, chunk):
    feats, cols = weight.shape
    count, slots = coefs.shape
    high = feats // CH
    view = weight.reshape(high, CH, cols)
    lanes = chunk * CH
    out = pl.pallas_call(
        total_kernel,
        out_shape=jax.ShapeDtypeStruct(view.shape, F32),
        grid=(CH // chunk,),
        in_specs=[
            pl.BlockSpec((count, slots), lambda c: (0, 0)),
            pl.BlockSpec((count, lanes), lambda c: (0, c)),
            pl.BlockSpec((count, lanes), lambda c: (0, c)),
            pl.BlockSpec((high, chunk, cols), lambda c: (0, c, 0)),
        ],
        out_specs=pl.BlockSpec((high, chunk, cols), lambda c: (0, c, 0)),
        scratch_shapes=[
            pltpu.VMEM((slots, count), BF),
            pltpu.VMEM((slots, count), BF),
            pltpu.VMEM((cols // (2 * CH), high * chunk, 2 * CH), F32),
        ],
        cost_estimate=pl.CostEstimate(
            flops=6 * count * slots * CH * CH, bytes_accessed=8 * feats * cols, transcendentals=0
        ),
        name="total",
    )(coefs, w_high, w_low, view)
    return out.reshape(feats, cols)


def exchange(value, axis, size, bit):
    return lax.ppermute(value, axis, [(i, i ^ bit) for i in range(size)])


def body(reps, parts, activations, out_grad, weight, momentum, select):
    thirds = jnp.asarray(dct_thirds())
    me = lax.axis_index("rep").astype(jnp.int32)
    part = lax.axis_index("feat").astype(jnp.int32)

    pieces = {0: out_grad}
    bit = parts // 2
    while bit:
        for s in list(pieces):
            pieces[s | bit] = exchange(pieces[s], "feat", parts, bit)
        bit //= 2
    near = [pieces[s] for s in range(parts // 2)] if parts > 1 else [out_grad]
    far = [pieces[s] for s in range(parts // 2, parts)] if parts > 1 else []

    order = me ^ jnp.arange(reps, dtype=jnp.int32)
    w_high, w_low = make_tables(order, select, thirds, 8)

    shape = (activations.shape[0], activations.shape[1])
    half = len(near)
    top = part // half
    near_at = jnp.stack([top] + [(part % half) ^ s for s in range(half)])
    far_at = jnp.stack([top ^ 1] + [(part % half) ^ s for s in range(half)])
    in_grad = make_in_grad(near_at, near, weight, (shape, None), 256)

    where = jnp.stack([me] + [part ^ s for s in range(parts)])
    residual, own = make_grad(
        where, activations, near + far, momentum, select, thirds, 256
    )
    if far:
        in_grad = make_in_grad(far_at, far, weight, (shape, in_grad), 256)
    coefs = own
    bit = 1
    while bit < reps:
        coefs = jnp.concatenate([coefs, exchange(coefs, "rep", reps, bit)], axis=0)
        bit *= 2
    new_weight = make_total(coefs, w_high, w_low, weight, 8)
    return in_grad, residual, new_weight


def solution(mesh):
    reps, parts = mesh.shape["rep"], mesh.shape["feat"]
    assert reps & (reps - 1) == 0 and parts & (parts - 1) == 0
    in_specs = (
        P("rep", "feat"),
        P(("rep", "feat"), None),
        P("feat", None),
        P("rep", "feat", None),
        P(),
    )
    out_specs = (P("rep", "feat"), P("rep", "feat", None), P("feat", None))
    return jax.shard_map(
        functools.partial(body, reps, parts),
        mesh=mesh,
        in_specs=in_specs,
        out_specs=out_specs,
        check_vma=False,
    )
```

```python
import functools
import math

import jax
import jax.numpy as jnp
import numpy as np
from jax import lax
from jax.experimental import pallas as pl
from jax.experimental.pallas import tpu as pltpu
from jax.sharding import PartitionSpec as P

CH = 64
BF = jnp.bfloat16
F32 = jnp.float32
ANY = pl.BlockSpec(memory_space=pl.ANY)
VMEM = pl.BlockSpec(memory_space=pltpu.VMEM)

momentum_decay = 0.9
step_rate = 0.5


def dct_thirds():
    index = np.arange(CH, dtype=np.float64)
    table = np.cos(np.pi * (2.0 * index[None, :] + 1.0) * index[:, None] / (2.0 * CH))
    table = table * np.sqrt(2.0 / CH)
    table[0] *= np.sqrt(0.5)
    terms = []
    rest = table.astype(np.float32)
    for _ in range(3):
        term = rest.astype(BF)
        terms.append(term)
        rest = rest - term.astype(np.float32)
    return np.concatenate(terms, axis=0)


def split2(value):
    high = value.astype(BF)
    return high, (value - high.astype(F32)).astype(BF)


def dot(a, b, contract=((1,), (0,))):
    return lax.dot_general(a, b, (contract, ((), ())), preferred_element_type=F32)


def one_hots(row):
    n = row.shape[1]
    freq = lax.broadcasted_iota(jnp.int32, (3 * CH, n), 0) & (CH - 1)
    u = (freq == (row >> int(math.log2(CH)))).astype(F32).astype(BF)
    v = (freq == (row & (CH - 1))).astype(F32).astype(BF)
    return u, v


def kept_in_hbm(value):
    return pltpu.with_memory_space_constraint(value, pltpu.HBM)


def kept_in_vmem(value):
    return pltpu.with_memory_space_constraint(value, pltpu.VMEM)


def early_kernel(
    block, half, tokens,
    g1, g0_hbm, x_hbm, w_hbm, mom_hbm, sel_hbm, thirds_hbm,
    out_hbm, acc, x_far, w_all, vb, vt, ua, sel, thirds,
    g_near, x_near, stage, sem_w, sem_x, sem_m, sem_f, sem_o, sem_s,
):
    me = lax.axis_index("rep")
    part = lax.axis_index("feat")
    feats, cols = acc.shape
    each = g1.shape[0]
    near = g_near.shape[0]
    blocks = feats // block
    kept = sel.shape[1]
    top = part // half
    row0 = pl.multiple_of(top * near, near)
    far0 = pl.multiple_of((1 - top) * near, near)
    tall = block // CH
    w_copies, x_copies, m_copies, f_copies, o_copies = [], [], [], [], []
    for b in range(blocks):
        at = pl.ds(b * block, block)
        heights = pl.ds(b * tall, tall)
        rows = pl.ds(row0, near)
        copy = pltpu.make_async_copy
        w_copies.append(copy(w_hbm.at[heights], w_all.at[heights], sem_w.at[b]))
        x_copies.append(copy(x_hbm.at[rows, at], x_near.at[:, at], sem_x.at[b]))
        m_copies.append(copy(mom_hbm.at[0, at], acc.at[at], sem_m.at[b]))
        f_copies.append(copy(x_hbm.at[pl.ds(far0, near), at], x_far.at[:, at], sem_f.at[b]))
        o_copies.append(copy(stage.at[:, at], out_hbm.at[rows, at], sem_o.at[b]))
    slot = part - top * half
    own_rows = pl.ds(pl.multiple_of(slot * each, each), each)
    small = [
        pltpu.make_async_copy(sel_hbm, sel, sem_s.at[0]),
        pltpu.make_async_copy(thirds_hbm, thirds, sem_s.at[1]),
        pltpu.make_async_copy(g0_hbm, g_near.at[own_rows], sem_s.at[2]),
    ]
    for copy in small + w_copies:
        copy.start()

    g_near[pl.ds(pl.multiple_of((1 - slot) * each, each), each), :] = g1[...]

    for copy in small:
        copy.wait()
    row = sel[pl.ds(me, 1), :]
    u, _ = one_hots(jnp.concatenate([row] * (ua.shape[1] // kept), axis=1))
    ua[...] = dot(thirds[...], u, ((0,), (0,)))
    wide = vt.shape[1]
    _, v = one_hots(jnp.concatenate([row] * (wide // CH), axis=1))
    vv = dot(v, thirds[...], ((0,), (0,)))
    vv = jnp.concatenate([vv] * (wide // CH), axis=1)
    r = lax.broadcasted_iota(jnp.int32, vv.shape, 0) // kept
    c = lax.broadcasted_iota(jnp.int32, vv.shape, 1) // CH
    vv = jnp.where(r == c, vv, 0.0)
    v_high, v_low = split2(vv)
    vt[...] = jnp.concatenate([v_high, v_high, v_low], axis=0)
    v_high, v_low = split2(vv.T)
    vb[...] = jnp.concatenate([v_high, v_low], axis=1)

    g = g_near[...]
    for b in range(blocks):
        w_copies[b].wait()
        x_copies[b].start()
        m_copies[b].start()
        w = w_all[b * tall : (b + 1) * tall].reshape(block, cols)
        w_high, w_low = split2(w)
        at = slice(b * block, (b + 1) * block)
        stage[:, at] = dot(g, w_high, ((1,), (1,))) + dot(g, w_low, ((1,), (1,)))
        o_copies[b].start()
    for b in range(blocks):
        f_copies[b].start()
    for b in range(blocks):
        x_copies[b].wait()
        m_copies[b].wait()
        at = slice(b * block, (b + 1) * block)
        grad = dot(x_near[:, at], g, ((0,), (0,)))
        acc[at, :] = momentum_decay * acc[at, :] + grad / tokens
    for copy in f_copies + o_copies:
        copy.wait()


def early(half, partner, out_grad, activations, weight, momentum, select, thirds):
    tokens, feats = activations.shape
    cols = momentum.shape[2]
    near = tokens // 2
    kept = select.shape[1]
    block = 512
    wide = 4 * CH
    dma = pltpu.SemaphoreType.DMA((feats // block,))
    return pl.pallas_call(
        functools.partial(early_kernel, block, half, tokens),
        out_shape=[
            jax.ShapeDtypeStruct((tokens, feats), F32),
            pltpu.VMEM((feats, cols), F32),
            pltpu.VMEM((near, feats), BF),
            pltpu.VMEM((feats // CH, CH, cols), F32),
            pltpu.VMEM((wide, 2 * 4 * kept), BF),
            pltpu.VMEM((3 * 4 * kept, wide), BF),
            pltpu.VMEM((CH, 4 * kept), F32),
            pltpu.VMEM(select.shape, select.dtype),
            pltpu.VMEM(thirds.shape, thirds.dtype),
        ],
        in_specs=[VMEM] + [ANY] * 6,
        out_specs=[ANY] + [VMEM] * 8,
        scratch_shapes=[
            pltpu.VMEM((near, cols), BF),
            pltpu.VMEM((near, feats), BF),
            pltpu.VMEM((near, feats), F32),
            dma, dma, dma, dma, dma,
            pltpu.SemaphoreType.DMA((3,)),
        ],
        compiler_params=pltpu.CompilerParams(vmem_limit_bytes=16 << 20),
        cost_estimate=pl.CostEstimate(
            flops=6 * tokens * feats * cols, bytes_accessed=20 * feats * cols, transcendentals=0
        ),
        name="early",
    )(partner, out_grad, activations, weight, momentum, select, thirds)


def table_kernel(sel, thirds, t_high, t_low, u3, v2):
    me = lax.axis_index("rep")
    reps, kept = sel.shape
    for p in range(reps):
        u, v = one_hots(sel[pl.ds(me ^ p, 1), :])
        rows = slice(p * kept, (p + 1) * kept)
        uu = dot(u, thirds[...], ((0,), (0,)))
        vv = dot(v, thirds[...], ((0,), (0,)))
        u_high, rest = split2(uu)
        u_low = (uu - u_high.astype(F32) - rest.astype(F32)).astype(BF)
        u3[rows, :] = jnp.concatenate([u_high, rest, u_low], axis=1)
        v2[rows, :] = jnp.concatenate([vv, vv], axis=1)
    lanes = 8 * CH
    for chunk in range(CH * CH // lanes):
        r = lax.broadcasted_iota(jnp.int32, (3 * CH, lanes), 0) & (CH - 1)
        c = lax.broadcasted_iota(jnp.int32, (3 * CH, lanes), 1) // CH + chunk * (lanes // CH)
        spread = (r == c).astype(F32).astype(BF)
        prod = dot(u3[...], spread) * jnp.concatenate([v2[...]] * (lanes // (2 * CH)), axis=1)
        at = slice(chunk * lanes, (chunk + 1) * lanes)
        t_high[:, at], t_low[:, at] = split2(prod)


def tables(select, thirds):
    count = select.size
    return pl.pallas_call(
        table_kernel,
        out_shape=[pltpu.VMEM((count, CH * CH), BF)] * 2,
        in_specs=[VMEM] * 2,
        out_specs=[VMEM] * 2,
        scratch_shapes=[
            pltpu.VMEM((count, 3 * CH), BF),
            pltpu.VMEM((count, 2 * CH), F32),
        ],
        compiler_params=pltpu.CompilerParams(vmem_limit_bytes=8 << 20),
        cost_estimate=pl.CostEstimate(
            flops=512 * count * CH * CH, bytes_accessed=4 * count * CH * CH, transcendentals=0
        ),
        name="tables",
    )(select, thirds)


def middle_kernel(
    block, half, tokens, g2, g3, x_far, acc, vb, ua, m_ref, by_i, by_k, g_far
):
    part = lax.axis_index("feat")
    feats, cols = acc.shape
    each = g2.shape[0]
    wide, both = vb.shape
    lanes = both // 2
    slot = part % half
    g_far[pl.ds(pl.multiple_of(slot * each, each), each), :] = g2[...]
    g_far[pl.ds(pl.multiple_of((1 - slot) * each, each), each), :] = g3[...]
    g = g_far[...]
    tall = block // CH
    for b in range(feats // block):
        at = slice(b * block, (b + 1) * block)
        moment = acc[at, :] + dot(x_far[:, at], g, ((0,), (0,))) / tokens
        m_ref[at, :] = moment
        m_high, m_low = split2(moment)
        for j in range(cols // wide):
            cut = slice(j * wide, (j + 1) * wide)
            y = dot(m_high[:, cut], vb[...])
            y = y[:, :lanes] + y[:, lanes:] + dot(m_low[:, cut], vb[:, :lanes])
            y = y.reshape(tall, CH, lanes) * ua[...][None]
            by_i[b * tall : (b + 1) * tall, j * lanes : (j + 1) * lanes] = jnp.sum(y, axis=1)
    kept = by_k.shape[0]
    turned = by_i[...].T
    count = turned.shape[0] // kept
    by_k[...] = jnp.concatenate(
        [turned[j * kept : (j + 1) * kept] for j in range(count)], axis=1
    )


def middle(half, kept, pieces, x_far, acc, vb, ua):
    tokens = 2 * x_far.shape[0]
    feats, cols = acc.shape
    high, count = feats // CH, cols // CH
    return pl.pallas_call(
        functools.partial(middle_kernel, 512, half, tokens),
        out_shape=[
            pltpu.VMEM((feats, cols), F32),
            pltpu.VMEM((high, count * kept), F32),
            pltpu.VMEM((kept, count * high), F32),
        ],
        in_specs=[VMEM] * 6,
        out_specs=[VMEM] * 3,
        scratch_shapes=[pltpu.VMEM((tokens // 2, cols), BF)],
        compiler_params=pltpu.CompilerParams(vmem_limit_bytes=14 << 20),
        cost_estimate=pl.CostEstimate(
            flops=3 * tokens * feats * cols, bytes_accessed=8 * feats * cols, transcendentals=0
        ),
        name="middle",
    )(*pieces, x_far, acc, vb, ua)


def fill_kernel(block, shift, with_residual, *refs):
    if with_residual:
        m_ref, by_i, vt, ua, g_ref, w_all, before, out_hbm, res_hbm, stage, res, sem, sem_r = refs
    else:
        g_ref, w_all, before, out_hbm, stage, sem = refs
    part = lax.axis_index("feat")
    each, cols = g_ref.shape
    feats = stage.shape[1]
    tall = block // CH
    copies = []
    if with_residual:
        lanes, wide = vt.shape[0] // 3, vt.shape[1]
        for b in range(feats // block):
            at = slice(b * block, (b + 1) * block)
            for j in range(cols // wide):
                c = by_i[b * tall : (b + 1) * tall, j * lanes : (j + 1) * lanes]
                e = (c[:, None, :] * ua[...][None]).reshape(block, lanes)
                e_high, e_low = split2(e)
                back = dot(jnp.concatenate([e_high, e_low], axis=1), vt[: 2 * lanes])
                back += dot(e_high, vt[2 * lanes :])
                cut = slice(j * wide, (j + 1) * wide)
                res[at, cut] = m_ref[at, cut] - back
            copies.append(pltpu.make_async_copy(res.at[at], res_hbm.at[0, at], sem_r.at[b]))
            copies[-1].start()
    row0 = pl.multiple_of((part ^ shift) * each, each)
    g = g_ref[...]
    for b in range(feats // block):
        w = w_all[b * tall : (b + 1) * tall].reshape(block, cols)
        w_high, w_low = split2(w)
        at = slice(b * block, (b + 1) * block)
        stage[:, at] = dot(g, w_high, ((1,), (1,))) + dot(g, w_low, ((1,), (1,)))
        copies.append(
            pltpu.make_async_copy(stage.at[:, at], out_hbm.at[pl.ds(row0, each), at], sem.at[b])
        )
        copies[-1].start()
    for copy in copies:
        copy.wait()


def fill(shift, piece, w_all, in_grad, residual_args=()):
    tokens, feats = in_grad.shape
    each, cols = piece.shape
    block = 512
    dma = pltpu.SemaphoreType.DMA((feats // block,))
    out_shape = [jax.ShapeDtypeStruct((tokens, feats), F32)]
    scratch = [pltpu.VMEM((each, feats), F32), dma]
    if residual_args:
        out_shape.append(jax.ShapeDtypeStruct((1, feats, cols), F32))
        scratch = [scratch[0], pltpu.VMEM((feats, cols), F32), dma, dma]
    args = [*residual_args, piece, w_all, in_grad]
    return pl.pallas_call(
        functools.partial(fill_kernel, block, shift, bool(residual_args)),
        out_shape=out_shape,
        in_specs=[VMEM] * (len(args) - 1) + [ANY],
        out_specs=[ANY] * len(out_shape),
        scratch_shapes=scratch,
        input_output_aliases={len(args) - 1: 0},
        compiler_params=pltpu.CompilerParams(vmem_limit_bytes=14 << 20),
        cost_estimate=pl.CostEstimate(
            flops=4 * each * feats * cols, bytes_accessed=4 * each * feats, transcendentals=0
        ),
        name="fill",
    )(*args)


def total_kernel(chunk, parts, *refs):
    coefs = refs[:parts]
    t_high, t_low, w_all, out_hbm, stage, sums, sem = refs[parts:]
    high, _, cols = w_all.shape
    coef = jnp.concatenate([c[...] for c in coefs], axis=0)
    c_high, c_low = split2(coef.T)
    slots = c_high.shape[0]
    c_both = jnp.concatenate([c_high, c_low], axis=0)
    left = lax.broadcasted_iota(jnp.int32, (high, 2 * CH), 1) < CH
    copies = []
    lanes = chunk * CH
    for b in range(CH // chunk):
        at = slice(b * lanes, (b + 1) * lanes)
        total = dot(c_both, t_high[:, at])
        total = total[:slots] + total[slots:] + dot(c_high, t_low[:, at])
        for p in range(chunk // 2):
            part = slice(p * 2 * CH, (p + 1) * 2 * CH)
            for q in range(cols // (2 * CH)):
                even = total[(2 * q) * high : (2 * q + 1) * high, part]
                odd = total[(2 * q + 1) * high : (2 * q + 2) * high, part]
                first = jnp.where(left, even, pltpu.roll(odd, CH, 1))
                second = jnp.where(left, pltpu.roll(even, CH, 1), odd)
                sums[b % 2, q, pl.ds(2 * p, high, stride=chunk), :] = first
                sums[b % 2, q, pl.ds(2 * p + 1, high, stride=chunk), :] = second
        rows = slice(b * chunk, (b + 1) * chunk)
        for q in range(cols // (2 * CH)):
            cut = slice(q * 2 * CH, (q + 1) * 2 * CH)
            part = sums[b % 2, q].reshape(high, chunk, 2 * CH)
            stage[:, rows, cut] = w_all[:, rows, cut] - step_rate * part
        copy = pltpu.make_async_copy(stage.at[:, rows], out_hbm.at[:, rows], sem.at[b])
        copy.start()
        copies.append(copy)
    for copy in copies:
        copy.wait()


def total_of(coefs, t_high, t_low, w_all):
    high, _, cols = w_all.shape
    chunk = 8
    return pl.pallas_call(
        functools.partial(total_kernel, chunk, len(coefs)),
        out_shape=jax.ShapeDtypeStruct(w_all.shape, F32),
        in_specs=[VMEM] * (len(coefs) + 3),
        out_specs=ANY,
        scratch_shapes=[
            pltpu.VMEM(w_all.shape, F32),
            pltpu.VMEM((2, cols // (2 * CH), high * chunk, 2 * CH), F32),
            pltpu.SemaphoreType.DMA((CH // chunk,)),
        ],
        compiler_params=pltpu.CompilerParams(vmem_limit_bytes=14 << 20),
        cost_estimate=pl.CostEstimate(
            flops=6 * t_high.size * coefs[0].shape[1], bytes_accessed=8 * w_all.size, transcendentals=0
        ),
        name="total",
    )(*coefs, t_high, t_low, w_all).reshape(high * CH, cols)


def exchange(value, axis, size, bit):
    return lax.ppermute(value, axis, [(i, i ^ bit) for i in range(size)])


def body(reps, parts, activations, out_grad, weight, momentum, select):
    thirds = jnp.asarray(dct_thirds())
    feats, cols = weight.shape
    kept = select.shape[1]
    half = parts // 2
    tie = lax.optimization_barrier
    heights = weight.reshape(feats // CH, CH, cols)
    hbm = [kept_in_hbm(a) for a in (out_grad, activations, heights, momentum, select, thirds)]

    partner = exchange(out_grad, "feat", parts, 1)
    across = exchange(out_grad, "feat", parts, half)
    in_grad, acc, x_far, w_all, vb, vt, ua, select, thirds = early(
        half, kept_in_vmem(partner), *hbm
    )
    across, acc = tie((across, acc))
    last = exchange(across, "feat", parts, 1)
    select, acc = tie((select, acc))
    t_high, t_low = tables(select, thirds)
    last, t_high, t_low = tie((last, t_high, t_low))
    m, by_i, by_k = middle(half, kept, [across, last], x_far, acc, vb, ua)

    first = exchange(by_k, "rep", reps, 1)
    (in_grad,) = fill(half | 1, last, w_all, in_grad)
    first, in_grad = tie((first, in_grad))
    coefs = jnp.concatenate([by_k, first], axis=0)
    coefs, m = tie((coefs, m))
    others = [exchange(coefs, "rep", reps, bit) for bit in range(2, reps, 2)]
    in_grad, residual = fill(half, across, w_all, in_grad, (m, by_i, vt, ua))
    *others, in_grad, residual = tie((*others, in_grad, residual))
    new_weight = total_of([coefs, *others], t_high, t_low, w_all)
    return in_grad, residual, new_weight


def solution(mesh):
    reps, parts = mesh.shape["rep"], mesh.shape["feat"]
    assert reps & (reps - 1) == 0 and reps >= 8 and parts == 4
    in_specs = (
        P("rep", "feat"),
        P(("rep", "feat"), None),
        P("feat", None),
        P("rep", "feat", None),
        P(),
    )
    out_specs = (P("rep", "feat"), P("rep", "feat", None), P("feat", None))
    return jax.shard_map(
        functools.partial(body, reps, parts),
        mesh=mesh,
        in_specs=in_specs,
        out_specs=out_specs,
        check_vma=False,
    )
```

```python
import functools
import math

import jax
import jax.numpy as jnp
import numpy as np
from jax import lax
from jax.experimental import pallas as pl
from jax.experimental.pallas import tpu as pltpu
from jax.sharding import PartitionSpec as P

CH = 64
BF = jnp.bfloat16
F32 = jnp.float32
ANY = pl.BlockSpec(memory_space=pl.ANY)
VMEM = pl.BlockSpec(memory_space=pltpu.VMEM)

momentum_decay = 0.9
step_rate = 0.5


def dct_thirds():
    index = np.arange(CH, dtype=np.float64)
    table = np.cos(np.pi * (2.0 * index[None, :] + 1.0) * index[:, None] / (2.0 * CH))
    table = table * np.sqrt(2.0 / CH)
    table[0] *= np.sqrt(0.5)
    terms = []
    rest = table.astype(np.float32)
    for _ in range(3):
        term = rest.astype(BF)
        terms.append(term)
        rest = rest - term.astype(np.float32)
    return np.concatenate(terms, axis=0)


def split2(value):
    high = value.astype(BF)
    return high, (value - high.astype(F32)).astype(BF)


def dot(a, b, contract=((1,), (0,))):
    return lax.dot_general(a, b, (contract, ((), ())), preferred_element_type=F32)


def one_hots(row):
    n = row.shape[1]
    freq = lax.broadcasted_iota(jnp.int32, (3 * CH, n), 0) & (CH - 1)
    u = (freq == (row >> int(math.log2(CH)))).astype(F32).astype(BF)
    v = (freq == (row & (CH - 1))).astype(F32).astype(BF)
    return u, v


def kept_in_hbm(value):
    return pltpu.with_memory_space_constraint(value, pltpu.HBM)


def kept_in_vmem(value):
    return pltpu.with_memory_space_constraint(value, pltpu.VMEM)


def fill_tables(order, me, sel, thirds, t_high, t_low, u3, v2):
    reps, kept = sel.shape
    for p, turn in enumerate(order):
        u, v = one_hots(sel[pl.ds(me ^ turn, 1), :])
        rows = slice(p * kept, (p + 1) * kept)
        uu = dot(u, thirds[...], ((0,), (0,)))
        vv = dot(v, thirds[...], ((0,), (0,)))
        u_high, rest = split2(uu)
        u_low = (uu - u_high.astype(F32) - rest.astype(F32)).astype(BF)
        u3[rows, :] = jnp.concatenate([u_high, rest, u_low], axis=1)
        v2[rows, :] = jnp.concatenate([vv, vv], axis=1)
    lanes = 8 * CH
    for chunk in range(CH * CH // lanes):
        r = lax.broadcasted_iota(jnp.int32, (3 * CH, lanes), 0) & (CH - 1)
        c = lax.broadcasted_iota(jnp.int32, (3 * CH, lanes), 1) // CH + chunk * (lanes // CH)
        spread = (r == c).astype(F32).astype(BF)
        prod = dot(u3[...], spread) * jnp.concatenate([v2[...]] * (lanes // (2 * CH)), axis=1)
        at = slice(chunk * lanes, (chunk + 1) * lanes)
        t_high[:, at], t_low[:, at] = split2(prod)


def early_kernel(
    block, half, tokens,
    g1, g0_hbm, x_hbm, w_hbm, mom_hbm, sel_hbm, thirds_hbm,
    out_hbm, acc, x_far, w_all, sel, thirds,
    g_near, x_near, stage, sem_w, sem_x, sem_m, sem_f, sem_o, sem_s,
):
    part = lax.axis_index("feat")
    feats, cols = acc.shape
    each = g1.shape[0]
    near = g_near.shape[0]
    blocks = feats // block
    top = part // half
    row0 = pl.multiple_of(top * near, near)
    far0 = pl.multiple_of((1 - top) * near, near)
    tall = block // CH
    w_copies, x_copies, m_copies, f_copies, o_copies = [], [], [], [], []
    for b in range(blocks):
        at = pl.ds(b * block, block)
        heights = pl.ds(b * tall, tall)
        rows = pl.ds(row0, near)
        copy = pltpu.make_async_copy
        w_copies.append(copy(w_hbm.at[heights], w_all.at[heights], sem_w.at[b]))
        x_copies.append(copy(x_hbm.at[rows, at], x_near.at[:, at], sem_x.at[b]))
        m_copies.append(copy(mom_hbm.at[0, at], acc.at[at], sem_m.at[b]))
        f_copies.append(copy(x_hbm.at[pl.ds(far0, near), at], x_far.at[:, at], sem_f.at[b]))
        o_copies.append(copy(stage.at[:, at], out_hbm.at[rows, at], sem_o.at[b]))
    slot = part - top * half
    own_rows = pl.ds(pl.multiple_of(slot * each, each), each)
    small = [
        pltpu.make_async_copy(sel_hbm, sel, sem_s.at[0]),
        pltpu.make_async_copy(thirds_hbm, thirds, sem_s.at[1]),
        pltpu.make_async_copy(g0_hbm, g_near.at[own_rows], sem_s.at[2]),
    ]
    for copy in small[2:] + w_copies + small[:2]:
        copy.start()

    g_near[pl.ds(pl.multiple_of((1 - slot) * each, each), each), :] = g1[...]

    small[2].wait()
    g = g_near[...]
    for b in range(blocks):
        w_copies[b].wait()
        if b == 0:
            for copy in x_copies + m_copies:
                copy.start()
        w = w_all[b * tall : (b + 1) * tall].reshape(block, cols)
        w_high, w_low = split2(w)
        at = slice(b * block, (b + 1) * block)
        stage[:, at] = dot(g, w_high, ((1,), (1,))) + dot(g, w_low, ((1,), (1,)))
        o_copies[b].start()
        f_copies[b].start()
    for b in range(blocks):
        x_copies[b].wait()
        m_copies[b].wait()
        at = slice(b * block, (b + 1) * block)
        grad = dot(x_near[:, at], g, ((0,), (0,)))
        acc[at, :] = momentum_decay * acc[at, :] + grad / tokens
    for copy in small[:2] + f_copies + o_copies:
        copy.wait()


def early(half, partner, out_grad, activations, weight, momentum, select, thirds):
    tokens, feats = activations.shape
    cols = momentum.shape[2]
    near = tokens // 2
    block = 512
    dma = pltpu.SemaphoreType.DMA((feats // block,))
    return pl.pallas_call(
        functools.partial(early_kernel, block, half, tokens),
        out_shape=[
            jax.ShapeDtypeStruct((tokens, feats), F32),
            pltpu.VMEM((feats, cols), F32),
            pltpu.VMEM((near, feats), BF),
            pltpu.VMEM((feats // CH, CH, cols), F32),
            pltpu.VMEM(select.shape, select.dtype),
            pltpu.VMEM(thirds.shape, thirds.dtype),
        ],
        in_specs=[VMEM] + [ANY] * 6,
        out_specs=[ANY] + [VMEM] * 5,
        scratch_shapes=[
            pltpu.VMEM((near, cols), BF),
            pltpu.VMEM((near, feats), BF),
            pltpu.VMEM((near, feats), F32),
            dma, dma, dma, dma, dma,
            pltpu.SemaphoreType.DMA((3,)),
        ],
        compiler_params=pltpu.CompilerParams(vmem_limit_bytes=16 << 20),
        cost_estimate=pl.CostEstimate(
            flops=6 * tokens * feats * cols, bytes_accessed=20 * feats * cols, transcendentals=0
        ),
        name="early",
    )(partner, out_grad, activations, weight, momentum, select, thirds)


def partial_kernel(block, half, tokens, g_ref, x_far, acc, sel, thirds, out, vb, vt, ua):
    me = lax.axis_index("rep")
    kept = sel.shape[1]
    row = sel[pl.ds(me, 1), :]
    u, _ = one_hots(jnp.concatenate([row] * (ua.shape[1] // kept), axis=1))
    ua[...] = dot(thirds[...], u, ((0,), (0,)))
    wide = vt.shape[1]
    _, v = one_hots(jnp.concatenate([row] * (wide // CH), axis=1))
    vv = dot(v, thirds[...], ((0,), (0,)))
    vv = jnp.concatenate([vv] * (wide // CH), axis=1)
    r = lax.broadcasted_iota(jnp.int32, vv.shape, 0) // kept
    c = lax.broadcasted_iota(jnp.int32, vv.shape, 1) // CH
    vv = jnp.where(r == c, vv, 0.0)
    v_high, v_low = split2(vv)
    vt[...] = jnp.concatenate([v_high, v_high, v_low], axis=0)
    v_high, v_low = split2(vv.T)
    vb[...] = jnp.concatenate([v_high, v_low], axis=1)

    each = g_ref.shape[0]
    slot = lax.axis_index("feat") % half
    rows = pl.ds(pl.multiple_of(slot * each, each), each)
    g = g_ref[...]
    for b in range(acc.shape[0] // block):
        at = slice(b * block, (b + 1) * block)
        out[at, :] = acc[at, :] + dot(x_far[rows, at], g, ((0,), (0,))) / tokens


def partial_grad(half, piece, x_far, acc, select, thirds):
    feats, cols = acc.shape
    kept = select.shape[1]
    wide = 4 * CH
    return pl.pallas_call(
        functools.partial(partial_kernel, 512, half, 2 * x_far.shape[0]),
        out_shape=[
            pltpu.VMEM((feats, cols), F32),
            pltpu.VMEM((wide, 2 * 4 * kept), BF),
            pltpu.VMEM((3 * 4 * kept, wide), BF),
            pltpu.VMEM((CH, 4 * kept), F32),
        ],
        in_specs=[VMEM] * 5,
        out_specs=[VMEM] * 4,
        compiler_params=pltpu.CompilerParams(vmem_limit_bytes=8 << 20),
        cost_estimate=pl.CostEstimate(
            flops=2 * piece.shape[0] * feats * cols, bytes_accessed=1 << 20, transcendentals=0
        ),
        name="partial",
    )(piece, x_far, acc, select, thirds)


def middle_kernel(block, half, tokens, pieces, *refs):
    gs = refs[:pieces]
    x_far, acc, vb, ua, m_ref, by_i, by_k = refs[pieces : pieces + 7]
    feats, cols = acc.shape
    each = gs[0].shape[0]
    wide, both = vb.shape
    lanes = both // 2
    slot = lax.axis_index("feat") % half
    if pieces > 1:
        g_far = refs[-1]
        g_far[pl.ds(pl.multiple_of(slot * each, each), each), :] = gs[0][...]
        g_far[pl.ds(pl.multiple_of((1 - slot) * each, each), each), :] = gs[1][...]
        g = g_far[...]
        rows = pl.ds(0, 2 * each)
    else:
        g = gs[0][...]
        rows = pl.ds(pl.multiple_of((1 - slot) * each, each), each)
    tall = block // CH
    for b in range(feats // block):
        at = slice(b * block, (b + 1) * block)
        moment = acc[at, :] + dot(x_far[rows, at], g, ((0,), (0,))) / tokens
        m_ref[at, :] = moment
        m_high, m_low = split2(moment)
        for j in range(cols // wide):
            cut = slice(j * wide, (j + 1) * wide)
            y = dot(m_high[:, cut], vb[...])
            y = y[:, :lanes] + y[:, lanes:] + dot(m_low[:, cut], vb[:, :lanes])
            y = y.reshape(tall, CH, lanes) * ua[...][None]
            by_i[b * tall : (b + 1) * tall, j * lanes : (j + 1) * lanes] = jnp.sum(y, axis=1)
    kept = by_k.shape[0]
    turned = by_i[...].T
    count = turned.shape[0] // kept
    by_k[...] = jnp.concatenate(
        [turned[j * kept : (j + 1) * kept] for j in range(count)], axis=1
    )


def middle(half, kept, pieces, x_far, acc, vb, ua):
    tokens = 2 * x_far.shape[0]
    feats, cols = acc.shape
    high, count = feats // CH, cols // CH
    scratch = [pltpu.VMEM((tokens // 2, cols), BF)] if len(pieces) > 1 else []
    return pl.pallas_call(
        functools.partial(middle_kernel, 512, half, tokens, len(pieces)),
        out_shape=[
            pltpu.VMEM((feats, cols), F32),
            pltpu.VMEM((high, count * kept), F32),
            pltpu.VMEM((kept, count * high), F32),
        ],
        in_specs=[VMEM] * (len(pieces) + 4),
        out_specs=[VMEM] * 3,
        scratch_shapes=scratch,
        compiler_params=pltpu.CompilerParams(vmem_limit_bytes=14 << 20),
        cost_estimate=pl.CostEstimate(
            flops=3 * tokens * feats * cols, bytes_accessed=8 * feats * cols, transcendentals=0
        ),
        name="middle",
    )(*pieces, x_far, acc, vb, ua)


def residual_kernel(
    block, order, m_ref, by_i, vt, ua, sel, thirds, res, t_high, t_low, u3, v2
):
    feats, cols = m_ref.shape
    tall = block // CH
    lanes, wide = vt.shape[0] // 3, vt.shape[1]
    for b in range(feats // block):
        at = slice(b * block, (b + 1) * block)
        for j in range(cols // wide):
            c = by_i[b * tall : (b + 1) * tall, j * lanes : (j + 1) * lanes]
            e = (c[:, None, :] * ua[...][None]).reshape(block, lanes)
            e_high, e_low = split2(e)
            back = dot(jnp.concatenate([e_high, e_low], axis=1), vt[: 2 * lanes])
            back += dot(e_high, vt[2 * lanes :])
            cut = slice(j * wide, (j + 1) * wide)
            res[at, cut] = m_ref[at, cut] - back
    fill_tables(order, lax.axis_index("rep"), sel, thirds, t_high, t_low, u3, v2)


def residual_of(order, m, by_i, vt, ua, select, thirds):
    feats, cols = m.shape
    count = select.size
    return pl.pallas_call(
        functools.partial(residual_kernel, 512, order),
        out_shape=[
            pltpu.VMEM((feats, cols), F32),
            pltpu.VMEM((count, CH * CH), BF),
            pltpu.VMEM((count, CH * CH), BF),
        ],
        in_specs=[VMEM] * 6,
        out_specs=[VMEM] * 3,
        scratch_shapes=[
            pltpu.VMEM((count, 3 * CH), BF),
            pltpu.VMEM((count, 2 * CH), F32),
        ],
        compiler_params=pltpu.CompilerParams(vmem_limit_bytes=8 << 20),
        cost_estimate=pl.CostEstimate(
            flops=1000 * feats * cols, bytes_accessed=1 << 20, transcendentals=0
        ),
        name="residual",
    )(m, by_i, vt, ua, select, thirds)


def late_kernel(
    block, half, res, g2, g3, w_all, before, res_hbm, out_hbm, g_far, stage, sem, sem_r
):
    part = lax.axis_index("feat")
    each, cols = g2.shape
    far, feats = stage.shape
    tall = block // CH
    slot = part % half
    row0 = pl.multiple_of((1 - part // half) * far, far)
    copies = []
    for b in range(feats // block):
        at = pl.ds(b * block, block)
        copies.append(pltpu.make_async_copy(res.at[at], res_hbm.at[0, at], sem_r.at[b]))
        copies[-1].start()
    g_far[pl.ds(pl.multiple_of(slot * each, each), each), :] = g2[...]
    g_far[pl.ds(pl.multiple_of((1 - slot) * each, each), each), :] = g3[...]
    g = g_far[...]
    for b in range(feats // block):
        w = w_all[b * tall : (b + 1) * tall].reshape(block, cols)
        w_high, w_low = split2(w)
        at = slice(b * block, (b + 1) * block)
        stage[:, at] = dot(g, w_high, ((1,), (1,))) + dot(g, w_low, ((1,), (1,)))
        copies.append(
            pltpu.make_async_copy(stage.at[:, at], out_hbm.at[pl.ds(row0, far), at], sem.at[b])
        )
        copies[-1].start()
    for copy in copies:
        copy.wait()


def late(half, residual, pieces, w_all, in_grad):
    block = 512
    tokens, feats = in_grad.shape
    each, cols = pieces[0].shape
    dma = pltpu.SemaphoreType.DMA((feats // block,))
    return pl.pallas_call(
        functools.partial(late_kernel, block, half),
        out_shape=[
            jax.ShapeDtypeStruct((1, feats, cols), F32),
            jax.ShapeDtypeStruct(in_grad.shape, F32),
        ],
        in_specs=[VMEM] * 4 + [ANY],
        out_specs=[ANY] * 2,
        scratch_shapes=[
            pltpu.VMEM((2 * each, cols), BF),
            pltpu.VMEM((2 * each, feats), F32),
            dma,
            dma,
        ],
        input_output_aliases={4: 1},
        compiler_params=pltpu.CompilerParams(vmem_limit_bytes=14 << 20),
        cost_estimate=pl.CostEstimate(
            flops=8 * each * feats * cols, bytes_accessed=1 << 22, transcendentals=0
        ),
        name="late",
    )(residual, *pieces, w_all, in_grad)


def total_kernel(chunk, parts, *refs):
    coefs = refs[:parts]
    t_high, t_low, w_all, out_hbm, stage, sums, sem = refs[parts:]
    high, _, cols = w_all.shape
    coef = jnp.concatenate([c[...] for c in coefs], axis=0)
    c_high, c_low = split2(coef.T)
    slots = c_high.shape[0]
    c_both = jnp.concatenate([c_high, c_low], axis=0)
    left = lax.broadcasted_iota(jnp.int32, (high, 2 * CH), 1) < CH
    copies = []
    lanes = chunk * CH
    for b in range(CH // chunk):
        at = slice(b * lanes, (b + 1) * lanes)
        total = dot(c_both, t_high[:, at])
        total = total[:slots] + total[slots:] + dot(c_high, t_low[:, at])
        for p in range(chunk // 2):
            part = slice(p * 2 * CH, (p + 1) * 2 * CH)
            for q in range(cols // (2 * CH)):
                even = total[(2 * q) * high : (2 * q + 1) * high, part]
                odd = total[(2 * q + 1) * high : (2 * q + 2) * high, part]
                first = jnp.where(left, even, pltpu.roll(odd, CH, 1))
                second = jnp.where(left, pltpu.roll(even, CH, 1), odd)
                sums[b % 2, q, pl.ds(2 * p, high, stride=chunk), :] = first
                sums[b % 2, q, pl.ds(2 * p + 1, high, stride=chunk), :] = second
        rows = slice(b * chunk, (b + 1) * chunk)
        for q in range(cols // (2 * CH)):
            cut = slice(q * 2 * CH, (q + 1) * 2 * CH)
            part = sums[b % 2, q].reshape(high, chunk, 2 * CH)
            stage[:, rows, cut] = w_all[:, rows, cut] - step_rate * part
        copy = pltpu.make_async_copy(stage.at[:, rows], out_hbm.at[:, rows], sem.at[b])
        copy.start()
        copies.append(copy)
    for copy in copies:
        copy.wait()


def total_of(coefs, t_high, t_low, w_all):
    high, _, cols = w_all.shape
    chunk = 8
    return pl.pallas_call(
        functools.partial(total_kernel, chunk, len(coefs)),
        out_shape=jax.ShapeDtypeStruct(w_all.shape, F32),
        in_specs=[VMEM] * (len(coefs) + 3),
        out_specs=ANY,
        scratch_shapes=[
            pltpu.VMEM(w_all.shape, F32),
            pltpu.VMEM((2, cols // (2 * CH), high * chunk, 2 * CH), F32),
            pltpu.SemaphoreType.DMA((CH // chunk,)),
        ],
        compiler_params=pltpu.CompilerParams(vmem_limit_bytes=14 << 20),
        cost_estimate=pl.CostEstimate(
            flops=6 * t_high.size * coefs[0].shape[1], bytes_accessed=8 * w_all.size, transcendentals=0
        ),
        name="total",
    )(*coefs, t_high, t_low, w_all).reshape(high * CH, cols)


def exchange(value, axis, size, bit):
    return lax.ppermute(value, axis, [(i, i ^ bit) for i in range(size)])


def body(reps, parts, activations, out_grad, weight, momentum, select):
    thirds = jnp.asarray(dct_thirds())
    feats, cols = weight.shape
    kept = select.shape[1]
    half = parts // 2
    tie = lax.optimization_barrier
    heights = weight.reshape(feats // CH, CH, cols)
    hbm = [kept_in_hbm(a) for a in (out_grad, activations, heights, momentum, select, thirds)]
    far_rep = reps // 2
    turns = list(range(1, far_rep))
    order = tuple(turn ^ end for turn in [0, *turns] for end in (0, far_rep))

    partner = exchange(out_grad, "feat", parts, 1)
    across = exchange(out_grad, "feat", parts, half)
    in_grad, acc, x_far, w_all, select, thirds = early(half, kept_in_vmem(partner), *hbm)
    across, acc = tie((across, acc))
    last = exchange(across, "feat", parts, 1)
    acc, vb, vt, ua = partial_grad(half, across, x_far, acc, select, thirds)
    last, acc = tie((last, acc))
    m, by_i, by_k = middle(half, kept, [last], x_far, acc, vb, ua)

    first = exchange(by_k, "rep", reps, far_rep)
    residual, t_high, t_low = residual_of(order, m, by_i, vt, ua, select, thirds)
    first, residual = tie((first, residual))
    coefs = jnp.concatenate([by_k, first], axis=0)
    coefs, last, residual = tie((coefs, last, residual))
    others = [exchange(coefs, "rep", reps, turn) for turn in turns]
    residual, in_grad = late(half, residual, [across, last], w_all, in_grad)
    *others, in_grad, residual = tie((*others, in_grad, residual))
    new_weight = total_of([coefs, *others], t_high, t_low, w_all)
    return in_grad, residual, new_weight


def solution(mesh):
    reps, parts = mesh.shape["rep"], mesh.shape["feat"]
    assert reps & (reps - 1) == 0 and reps >= 8 and parts == 4
    in_specs = (
        P("rep", "feat"),
        P(("rep", "feat"), None),
        P("feat", None),
        P("rep", "feat", None),
        P(),
    )
    out_specs = (P("rep", "feat"), P("rep", "feat", None), P("feat", None))
    return jax.shard_map(
        functools.partial(body, reps, parts),
        mesh=mesh,
        in_specs=in_specs,
        out_specs=out_specs,
        check_vma=False,
    )
```

```python
import functools
import math

import jax
import jax.numpy as jnp
import numpy as np
from jax import lax
from jax.experimental import pallas as pl
from jax.experimental.pallas import tpu as pltpu
from jax.sharding import PartitionSpec as P

CH = 64
BF = jnp.bfloat16
F32 = jnp.float32
ANY = pl.BlockSpec(memory_space=pl.ANY)
VMEM = pl.BlockSpec(memory_space=pltpu.VMEM)

momentum_decay = 0.9
step_rate = 0.5


def dct_thirds():
    index = np.arange(CH, dtype=np.float64)
    table = np.cos(np.pi * (2.0 * index[None, :] + 1.0) * index[:, None] / (2.0 * CH))
    table = table * np.sqrt(2.0 / CH)
    table[0] *= np.sqrt(0.5)
    terms = []
    rest = table.astype(np.float32)
    for _ in range(3):
        term = rest.astype(BF)
        terms.append(term)
        rest = rest - term.astype(np.float32)
    return np.concatenate(terms, axis=0)


def split2(value):
    high = value.astype(BF)
    return high, (value - high.astype(F32)).astype(BF)


def dot(a, b, contract=((1,), (0,))):
    return lax.dot_general(a, b, (contract, ((), ())), preferred_element_type=F32)


def one_hots(row):
    n = row.shape[1]
    freq = lax.broadcasted_iota(jnp.int32, (3 * CH, n), 0) & (CH - 1)
    u = (freq == (row >> int(math.log2(CH)))).astype(F32).astype(BF)
    v = (freq == (row & (CH - 1))).astype(F32).astype(BF)
    return u, v


def kept_in_hbm(value):
    return pltpu.with_memory_space_constraint(value, pltpu.HBM)


def kept_in_vmem(value):
    return pltpu.with_memory_space_constraint(value, pltpu.VMEM)


def fill_factors(order, me, sel, thirds, u3, v2):
    kept = sel.shape[1]
    for p, turn in enumerate(order):
        u, v = one_hots(sel[pl.ds(me ^ turn, 1), :])
        rows = slice(p * kept, (p + 1) * kept)
        uu = dot(u, thirds[...], ((0,), (0,)))
        vv = dot(v, thirds[...], ((0,), (0,)))
        u_high, rest = split2(uu)
        u_low = (uu - u_high.astype(F32) - rest.astype(F32)).astype(BF)
        u3[rows, :] = jnp.concatenate([u_high, rest, u_low], axis=1)
        v2[rows, :] = jnp.concatenate([vv, vv], axis=1)


def fill_tables(t_high, t_low, u3, v2):
    lanes = 8 * CH
    for chunk in range(CH * CH // lanes):
        r = lax.broadcasted_iota(jnp.int32, (3 * CH, lanes), 0) & (CH - 1)
        c = lax.broadcasted_iota(jnp.int32, (3 * CH, lanes), 1) // CH + chunk * (lanes // CH)
        spread = (r == c).astype(F32).astype(BF)
        prod = dot(u3[...], spread) * jnp.concatenate([v2[...]] * (lanes // (2 * CH)), axis=1)
        at = slice(chunk * lanes, (chunk + 1) * lanes)
        t_high[:, at], t_low[:, at] = split2(prod)


def early_kernel(
    block, half, tokens,
    g1, g0_hbm, x_hbm, w_hbm, mom_hbm, sel_hbm, thirds_hbm,
    out_hbm, acc, x_far, w_all, sel, thirds,
    g_near, x_near, stage, sem_w, sem_x, sem_m, sem_f, sem_o, sem_s,
):
    part = lax.axis_index("feat")
    feats, cols = acc.shape
    each = g1.shape[0]
    near = g_near.shape[0]
    blocks = feats // block
    top = part // half
    row0 = pl.multiple_of(top * near, near)
    far0 = pl.multiple_of((1 - top) * near, near)
    tall = block // CH
    w_copies, x_copies, m_copies, f_copies, o_copies = [], [], [], [], []
    for b in range(blocks):
        at = pl.ds(b * block, block)
        heights = pl.ds(b * tall, tall)
        rows = pl.ds(row0, near)
        copy = pltpu.make_async_copy
        w_copies.append(copy(w_hbm.at[heights], w_all.at[heights], sem_w.at[b]))
        x_copies.append(copy(x_hbm.at[rows, at], x_near.at[:, at], sem_x.at[b]))
        m_copies.append(copy(mom_hbm.at[0, at], acc.at[at], sem_m.at[b]))
        f_copies.append(copy(x_hbm.at[pl.ds(far0, near), at], x_far.at[:, at], sem_f.at[b]))
        o_copies.append(copy(stage.at[:, at], out_hbm.at[rows, at], sem_o.at[b]))
    slot = part - top * half
    own_rows = pl.ds(pl.multiple_of(slot * each, each), each)
    small = [
        pltpu.make_async_copy(sel_hbm, sel, sem_s.at[0]),
        pltpu.make_async_copy(thirds_hbm, thirds, sem_s.at[1]),
        pltpu.make_async_copy(g0_hbm, g_near.at[own_rows], sem_s.at[2]),
    ]
    for copy in small[2:] + w_copies + small[:2]:
        copy.start()

    g_near[pl.ds(pl.multiple_of((1 - slot) * each, each), each), :] = g1[...]

    small[2].wait()
    g = g_near[...]
    for b in range(blocks):
        w_copies[b].wait()
        if b == 0:
            for copy in x_copies + m_copies:
                copy.start()
        w = w_all[b * tall : (b + 1) * tall].reshape(block, cols)
        w_high, w_low = split2(w)
        at = slice(b * block, (b + 1) * block)
        stage[:, at] = dot(g, w_high, ((1,), (1,))) + dot(g, w_low, ((1,), (1,)))
        o_copies[b].start()
        f_copies[b].start()
    for b in range(blocks):
        x_copies[b].wait()
        m_copies[b].wait()
        at = slice(b * block, (b + 1) * block)
        grad = dot(x_near[:, at], g, ((0,), (0,)))
        acc[at, :] = momentum_decay * acc[at, :] + grad / tokens
    for copy in small[:2] + f_copies + o_copies:
        copy.wait()


def early(half, partner, out_grad, activations, weight, momentum, select, thirds):
    tokens, feats = activations.shape
    cols = momentum.shape[2]
    near = tokens // 2
    block = feats
    dma = pltpu.SemaphoreType.DMA((feats // block,))
    return pl.pallas_call(
        functools.partial(early_kernel, block, half, tokens),
        out_shape=[
            jax.ShapeDtypeStruct((tokens, feats), F32),
            pltpu.VMEM((feats, cols), F32),
            pltpu.VMEM((near, feats), BF),
            pltpu.VMEM((feats // CH, CH, cols), F32),
            pltpu.VMEM(select.shape, select.dtype),
            pltpu.VMEM(thirds.shape, thirds.dtype),
        ],
        in_specs=[VMEM] + [ANY] * 6,
        out_specs=[ANY] + [VMEM] * 5,
        scratch_shapes=[
            pltpu.VMEM((near, cols), BF),
            pltpu.VMEM((near, feats), BF),
            pltpu.VMEM((near, feats), F32),
            dma, dma, dma, dma, dma,
            pltpu.SemaphoreType.DMA((3,)),
        ],
        compiler_params=pltpu.CompilerParams(vmem_limit_bytes=16 << 20),
        cost_estimate=pl.CostEstimate(
            flops=6 * tokens * feats * cols, bytes_accessed=20 * feats * cols, transcendentals=0
        ),
        name="early",
    )(partner, out_grad, activations, weight, momentum, select, thirds)


def partial_kernel(
    block, half, tokens, order, g_ref, x_far, acc, sel, thirds, out, vb, vt, ua, u3, v2
):
    me = lax.axis_index("rep")
    kept = sel.shape[1]
    row = sel[pl.ds(me, 1), :]
    u, _ = one_hots(jnp.concatenate([row] * (ua.shape[1] // kept), axis=1))
    ua[...] = dot(thirds[...], u, ((0,), (0,)))
    wide = vt.shape[1]
    _, v = one_hots(jnp.concatenate([row] * (wide // CH), axis=1))
    vv = dot(v, thirds[...], ((0,), (0,)))
    vv = jnp.concatenate([vv] * (wide // CH), axis=1)
    r = lax.broadcasted_iota(jnp.int32, vv.shape, 0) // kept
    c = lax.broadcasted_iota(jnp.int32, vv.shape, 1) // CH
    vv = jnp.where(r == c, vv, 0.0)
    v_high, v_low = split2(vv)
    vt[...] = jnp.concatenate([v_high, v_high, v_low], axis=0)
    v_high, v_low = split2(vv.T)
    vb[...] = jnp.concatenate([v_high, v_low], axis=1)

    each = g_ref.shape[0]
    slot = lax.axis_index("feat") % half
    rows = pl.ds(pl.multiple_of(slot * each, each), each)
    g = g_ref[...]
    for b in range(acc.shape[0] // block):
        at = slice(b * block, (b + 1) * block)
        out[at, :] = acc[at, :] + dot(x_far[rows, at], g, ((0,), (0,))) / tokens
    fill_factors(order, me, sel, thirds, u3, v2)


def partial_grad(half, order, piece, x_far, acc, select, thirds):
    feats, cols = acc.shape
    kept = select.shape[1]
    wide = 4 * CH
    return pl.pallas_call(
        functools.partial(partial_kernel, 512, half, 2 * x_far.shape[0], order),
        out_shape=[
            pltpu.VMEM((feats, cols), F32),
            pltpu.VMEM((wide, 2 * 4 * kept), BF),
            pltpu.VMEM((3 * 4 * kept, wide), BF),
            pltpu.VMEM((CH, 4 * kept), F32),
            pltpu.VMEM((select.size, 3 * CH), BF),
            pltpu.VMEM((select.size, 2 * CH), F32),
        ],
        in_specs=[VMEM] * 5,
        out_specs=[VMEM] * 6,
        compiler_params=pltpu.CompilerParams(vmem_limit_bytes=8 << 20),
        cost_estimate=pl.CostEstimate(
            flops=2 * piece.shape[0] * feats * cols, bytes_accessed=1 << 20, transcendentals=0
        ),
        name="partial",
    )(piece, x_far, acc, select, thirds)


def middle_kernel(block, half, tokens, pieces, *refs):
    gs = refs[:pieces]
    x_far, acc, vb, ua, m_ref, by_i, by_k = refs[pieces : pieces + 7]
    feats, cols = acc.shape
    each = gs[0].shape[0]
    wide, both = vb.shape
    lanes = both // 2
    slot = lax.axis_index("feat") % half
    if pieces > 1:
        g_far = refs[-1]
        g_far[pl.ds(pl.multiple_of(slot * each, each), each), :] = gs[0][...]
        g_far[pl.ds(pl.multiple_of((1 - slot) * each, each), each), :] = gs[1][...]
        g = g_far[...]
        rows = pl.ds(0, 2 * each)
    else:
        g = gs[0][...]
        rows = pl.ds(pl.multiple_of((1 - slot) * each, each), each)
    tall = block // CH
    for b in range(feats // block):
        at = slice(b * block, (b + 1) * block)
        moment = acc[at, :] + dot(x_far[rows, at], g, ((0,), (0,))) / tokens
        m_ref[at, :] = moment
        m_high, m_low = split2(moment)
        for j in range(cols // wide):
            cut = slice(j * wide, (j + 1) * wide)
            y = dot(m_high[:, cut], vb[...])
            y = y[:, :lanes] + y[:, lanes:] + dot(m_low[:, cut], vb[:, :lanes])
            y = y.reshape(tall, CH, lanes) * ua[...][None]
            by_i[b * tall : (b + 1) * tall, j * lanes : (j + 1) * lanes] = jnp.sum(y, axis=1)
    kept = by_k.shape[0]
    turned = by_i[...].T
    count = turned.shape[0] // kept
    by_k[...] = jnp.concatenate(
        [turned[j * kept : (j + 1) * kept] for j in range(count)], axis=1
    )


def middle(half, kept, pieces, x_far, acc, vb, ua):
    tokens = 2 * x_far.shape[0]
    feats, cols = acc.shape
    high, count = feats // CH, cols // CH
    scratch = [pltpu.VMEM((tokens // 2, cols), BF)] if len(pieces) > 1 else []
    return pl.pallas_call(
        functools.partial(middle_kernel, 512, half, tokens, len(pieces)),
        out_shape=[
            pltpu.VMEM((feats, cols), F32),
            pltpu.VMEM((high, count * kept), F32),
            pltpu.VMEM((kept, count * high), F32),
        ],
        in_specs=[VMEM] * (len(pieces) + 4),
        out_specs=[VMEM] * 3,
        scratch_shapes=scratch,
        compiler_params=pltpu.CompilerParams(vmem_limit_bytes=14 << 20),
        cost_estimate=pl.CostEstimate(
            flops=3 * tokens * feats * cols, bytes_accessed=8 * feats * cols, transcendentals=0
        ),
        name="middle",
    )(*pieces, x_far, acc, vb, ua)


def residual_kernel(
    block, m_ref, by_i, vt, ua, u3, v2, res, t_high, t_low
):
    feats, cols = m_ref.shape
    tall = block // CH
    lanes, wide = vt.shape[0] // 3, vt.shape[1]
    for b in range(feats // block):
        at = slice(b * block, (b + 1) * block)
        for j in range(cols // wide):
            c = by_i[b * tall : (b + 1) * tall, j * lanes : (j + 1) * lanes]
            e = (c[:, None, :] * ua[...][None]).reshape(block, lanes)
            e_high, e_low = split2(e)
            back = dot(jnp.concatenate([e_high, e_low], axis=1), vt[: 2 * lanes])
            back += dot(e_high, vt[2 * lanes :])
            cut = slice(j * wide, (j + 1) * wide)
            res[at, cut] = m_ref[at, cut] - back
    fill_tables(t_high, t_low, u3, v2)


def residual_of(m, by_i, vt, ua, u3, v2):
    feats, cols = m.shape
    count = u3.shape[0]
    return pl.pallas_call(
        functools.partial(residual_kernel, 512),
        out_shape=[
            pltpu.VMEM((feats, cols), F32),
            pltpu.VMEM((count, CH * CH), BF),
            pltpu.VMEM((count, CH * CH), BF),
        ],
        in_specs=[VMEM] * 6,
        out_specs=[VMEM] * 3,
        compiler_params=pltpu.CompilerParams(vmem_limit_bytes=8 << 20),
        cost_estimate=pl.CostEstimate(
            flops=1000 * feats * cols, bytes_accessed=1 << 20, transcendentals=0
        ),
        name="residual",
    )(m, by_i, vt, ua, u3, v2)


def late_kernel(
    block, half, res, g2, g3, w_all, before, res_hbm, out_hbm, g_far, stage, sem, sem_r
):
    part = lax.axis_index("feat")
    each, cols = g2.shape
    far, feats = stage.shape
    tall = block // CH
    slot = part % half
    row0 = pl.multiple_of((1 - part // half) * far, far)
    copies = []
    for b in range(feats // block):
        at = pl.ds(b * block, block)
        copies.append(pltpu.make_async_copy(res.at[at], res_hbm.at[0, at], sem_r.at[b]))
        copies[-1].start()
    g_far[pl.ds(pl.multiple_of(slot * each, each), each), :] = g2[...]
    g_far[pl.ds(pl.multiple_of((1 - slot) * each, each), each), :] = g3[...]
    g = g_far[...]
    for b in range(feats // block):
        w = w_all[b * tall : (b + 1) * tall].reshape(block, cols)
        w_high, w_low = split2(w)
        at = slice(b * block, (b + 1) * block)
        stage[:, at] = dot(g, w_high, ((1,), (1,))) + dot(g, w_low, ((1,), (1,)))
        copies.append(
            pltpu.make_async_copy(stage.at[:, at], out_hbm.at[pl.ds(row0, far), at], sem.at[b])
        )
        copies[-1].start()
    for copy in copies:
        copy.wait()


def late(half, residual, pieces, w_all, in_grad):
    block = 512
    tokens, feats = in_grad.shape
    each, cols = pieces[0].shape
    dma = pltpu.SemaphoreType.DMA((feats // block,))
    return pl.pallas_call(
        functools.partial(late_kernel, block, half),
        out_shape=[
            jax.ShapeDtypeStruct((1, feats, cols), F32),
            jax.ShapeDtypeStruct(in_grad.shape, F32),
        ],
        in_specs=[VMEM] * 4 + [ANY],
        out_specs=[ANY] * 2,
        scratch_shapes=[
            pltpu.VMEM((2 * each, cols), BF),
            pltpu.VMEM((2 * each, feats), F32),
            dma,
            dma,
        ],
        input_output_aliases={4: 1},
        compiler_params=pltpu.CompilerParams(vmem_limit_bytes=14 << 20),
        cost_estimate=pl.CostEstimate(
            flops=8 * each * feats * cols, bytes_accessed=1 << 22, transcendentals=0
        ),
        name="late",
    )(residual, *pieces, w_all, in_grad)


def total_kernel(chunk, parts, *refs):
    coefs = refs[:parts]
    t_high, t_low, w_all, out_hbm, stage, sums, sem = refs[parts:]
    high, _, cols = w_all.shape
    coef = jnp.concatenate([c[...] for c in coefs], axis=0)
    c_high, c_low = split2(coef.T)
    slots = c_high.shape[0]
    c_both = jnp.concatenate([c_high, c_low], axis=0)
    left = lax.broadcasted_iota(jnp.int32, (high, 2 * CH), 1) < CH
    copies = []
    lanes = chunk * CH
    def product(b):
        at = slice(b * lanes, (b + 1) * lanes)
        both = dot(c_both, t_high[:, at])
        return both[:slots] + both[slots:] + dot(c_high, t_low[:, at])

    def place(b, total):
        for p in range(chunk // 2):
            part = slice(p * 2 * CH, (p + 1) * 2 * CH)
            for q in range(cols // (2 * CH)):
                even = total[(2 * q) * high : (2 * q + 1) * high, part]
                odd = total[(2 * q + 1) * high : (2 * q + 2) * high, part]
                first = jnp.where(left, even, pltpu.roll(odd, CH, 1))
                second = jnp.where(left, pltpu.roll(even, CH, 1), odd)
                sums[b % 2, q, pl.ds(2 * p, high, stride=chunk), :] = first
                sums[b % 2, q, pl.ds(2 * p + 1, high, stride=chunk), :] = second
        rows = slice(b * chunk, (b + 1) * chunk)
        for q in range(cols // (2 * CH)):
            cut = slice(q * 2 * CH, (q + 1) * 2 * CH)
            part = sums[b % 2, q].reshape(high, chunk, 2 * CH)
            stage[:, rows, cut] = w_all[:, rows, cut] - step_rate * part
        copies.append(pltpu.make_async_copy(stage.at[:, rows], out_hbm.at[:, rows], sem.at[b]))
        copies[-1].start()

    ready = product(0)
    for b in range(1, CH // chunk):
        following = product(b)
        place(b - 1, ready)
        ready = following
    place(CH // chunk - 1, ready)
    for copy in copies:
        copy.wait()


def total_of(coefs, t_high, t_low, w_all):
    high, _, cols = w_all.shape
    chunk = 8
    return pl.pallas_call(
        functools.partial(total_kernel, chunk, len(coefs)),
        out_shape=jax.ShapeDtypeStruct(w_all.shape, F32),
        in_specs=[VMEM] * (len(coefs) + 3),
        out_specs=ANY,
        scratch_shapes=[
            pltpu.VMEM(w_all.shape, F32),
            pltpu.VMEM((2, cols // (2 * CH), high * chunk, 2 * CH), F32),
            pltpu.SemaphoreType.DMA((CH // chunk,)),
        ],
        compiler_params=pltpu.CompilerParams(vmem_limit_bytes=14 << 20),
        cost_estimate=pl.CostEstimate(
            flops=6 * t_high.size * coefs[0].shape[1], bytes_accessed=8 * w_all.size, transcendentals=0
        ),
        name="total",
    )(*coefs, t_high, t_low, w_all).reshape(high * CH, cols)


def exchange(value, axis, size, bit):
    return lax.ppermute(value, axis, [(i, i ^ bit) for i in range(size)])


def body(reps, parts, activations, out_grad, weight, momentum, select):
    thirds = jnp.asarray(dct_thirds())
    feats, cols = weight.shape
    kept = select.shape[1]
    half = parts // 2
    tie = lax.optimization_barrier
    heights = weight.reshape(feats // CH, CH, cols)
    hbm = [kept_in_hbm(a) for a in (out_grad, activations, heights, momentum, select, thirds)]
    far_rep = reps // 2
    turns = list(range(1, far_rep))
    order = tuple(turn ^ end for turn in [0, *turns] for end in (0, far_rep))

    partner = exchange(out_grad, "feat", parts, 1)
    across = exchange(out_grad, "feat", parts, half)
    in_grad, acc, x_far, w_all, select, thirds = early(half, kept_in_vmem(partner), *hbm)
    across, acc = tie((across, acc))
    last = exchange(across, "feat", parts, 1)
    acc, vb, vt, ua, u3, v2 = partial_grad(half, order, across, x_far, acc, select, thirds)
    last, acc = tie((last, acc))
    m, by_i, by_k = middle(half, kept, [last], x_far, acc, vb, ua)

    first = exchange(by_k, "rep", reps, far_rep)
    residual, t_high, t_low = residual_of(m, by_i, vt, ua, u3, v2)
    first, residual = tie((first, residual))
    coefs = jnp.concatenate([by_k, first], axis=0)
    coefs, last, residual = tie((coefs, last, residual))
    others = [exchange(coefs, "rep", reps, turn) for turn in turns]
    residual, in_grad = late(half, residual, [across, last], w_all, in_grad)
    *others, in_grad, residual = tie((*others, in_grad, residual))
    new_weight = total_of([coefs, *others], t_high, t_low, w_all)
    return in_grad, residual, new_weight


def solution(mesh):
    reps, parts = mesh.shape["rep"], mesh.shape["feat"]
    assert reps & (reps - 1) == 0 and reps >= 8 and parts == 4
    in_specs = (
        P("rep", "feat"),
        P(("rep", "feat"), None),
        P("feat", None),
        P("rep", "feat", None),
        P(),
    )
    out_specs = (P("rep", "feat"), P("rep", "feat", None), P("feat", None))
    return jax.shard_map(
        functools.partial(body, reps, parts),
        mesh=mesh,
        in_specs=in_specs,
        out_specs=out_specs,
        check_vma=False,
    )
```
